32 devices in a mesh: ctx: 8 (over y, x, core), ch: 4 (over z).
Axes of the slice: x: 2, y: 2, z: 4, core: 2. Of those that a mesh axis runs over, the one named last changes fastest.
Arguments:
- query_act: bfloat16 [2048, 8192], P('ctx', 'ch'), may hold values from -6 to 6
- key_act: bfloat16 [2048, 8192], P('ctx', 'ch'), may hold values from -6 to 6
- value_act: bfloat16 [2048, 8192], P('ctx', 'ch'), may hold values from -6 to 6
- out_grad: bfloat16 [2048, 8192], P('ctx', 'ch'), may hold values from -6 to 6
- out_weight: bfloat16 [8192, 8192], P('ctx', 'ch'), may hold values from -0.0625 to 0.0625
- token_mask: int32 [2048], P('ctx'), may hold values from 0 to 1, as said below
- decay_rate: float32 [16, 8192], P(None, 'ch'), may hold values from 4.8828125e-05 to 0.033
- residue: float32 [16, 8192], P(None, 'ch'), may hold values from -75 to 75
Outputs:
- query_grad: bfloat16 [2048, 8192], P('ctx', 'ch')
- key_grad: bfloat16 [2048, 8192], P('ctx', 'ch')
- value_grad: bfloat16 [2048, 8192], P('ctx', 'ch')
- filter_grad: float32 [16, 8192], P(None, 'ch')
The draws below stay inside these ranges and needn't reach their ends.
Inputs may be any that keep to these rules, and one draw needn't show every extreme that they name: `token_mask`: 1 marks a valid token; within each aligned run of 64 positions the valid tokens come first.
All inputs are finite; a program needn't handle non-finite values.
Results may differ from the reference program's by a relative error of at most 0.0015.
Values may be sent and summed in bfloat16 or wider, within the bound.
A program may use at most 192 MiB of HBM per device.

```python
import math
import jax
import jax.numpy as jnp
from jax import lax

D = 8192
MODES = 16
TOK_DEV = 256
RUN = 64
TOKENS = 2048


def draw_token_mask(key, part):
    span_count = TOKENS // TOK_DEV
    run_count = TOKENS // RUN
    density = jax.random.randint(jax.random.fold_in(key, 11), (span_count,), 0, 5)
    lengths = jax.random.randint(jax.random.fold_in(key, 12), (run_count,), 0, RUN + 1)
    span_of_run = jnp.arange(run_count) * RUN // TOK_DEV
    lengths = jnp.minimum(lengths * density[span_of_run] // 2, RUN)
    places = jnp.arange(TOKENS) % RUN
    return (places < jnp.repeat(lengths, RUN, total_repeat_length=TOKENS)).astype(jnp.int32)


def modal_pairs(key):
    pair_count = MODES // 2
    first_key, second_key, third_key = jax.random.split(key, 3)
    low_end = math.log(0.1 / TOKENS)
    high_end = math.log(0.03)
    base_rate = jnp.exp(jax.random.uniform(first_key, (pair_count, D), jnp.float32, low_end, high_end))
    ratio = jax.random.uniform(second_key, (pair_count, D), jnp.float32, 1.04, 1.08)
    strength = jax.random.truncated_normal(third_key, -3.0, 3.0, (pair_count, D), jnp.float32)
    paired_gain = strength / (ratio - 1.0)
    rates = jnp.stack([base_rate, base_rate * ratio], axis=1).reshape(MODES, D)
    residues = jnp.stack([paired_gain, -paired_gain], axis=1).reshape(MODES, D)
    return (rates, residues)


def draw_decay_rate(key, part):
    return modal_pairs(jax.random.fold_in(key, 31))[0]


def draw_residue(key, part):
    return modal_pairs(jax.random.fold_in(key, 31))[1]


def block_scale(rng, extent, pieces, low, largest):
    level, own = 1.0, jax.random.fold_in(rng, 6)
    for dim, parts in pieces:
        steps = jnp.exp(jax.random.uniform(jax.random.fold_in(own, dim), (parts,), jnp.float32, low / len(pieces), largest / len(pieces)))
        level = level * jnp.repeat(steps, extent[dim] // parts).reshape([-1 if axis == dim else 1 for axis in range(len(extent))])
    return level


def noise(stream_key, shape, scale, most, shards=(), kind=jnp.bfloat16):
    values = scale * jax.random.normal(stream_key, shape, jnp.float32)
    if shards:
        values = values * block_scale(stream_key, shape, shards, -0.22, 0.18)
    return jnp.clip(values, -most, most).astype(kind)


def setup_inputs(seed: int = 0) -> dict:
    key_list = jax.random.split(jax.random.key(seed), 9)
    return {
        "query_act": noise(key_list[0], (TOKENS, D), 1.0, 6.0, ((0, 8), (1, 4))),
        "key_act": noise(key_list[1], (TOKENS, D), 1.0, 6.0, ((0, 8), (1, 4))),
        "value_act": noise(key_list[2], (TOKENS, D), 1.0, 6.0, ((0, 8), (1, 4))),
        "out_grad": noise(key_list[3], (TOKENS, D), 1.0, 6.0, ((0, 8), (1, 4))),
        "out_weight": noise(key_list[4], (D, D), D ** -0.5, 0.0625, ((0, 8), (1, 4))),
        "token_mask": draw_token_mask(jax.random.fold_in(key_list[8], 71), 0),
        "decay_rate": draw_decay_rate(jax.random.fold_in(key_list[8], 71), 0),
        "residue": draw_residue(jax.random.fold_in(key_list[8], 71), 0),
    }


def reference(query_act, key_act, value_act, out_grad, out_weight, token_mask, decay_rate, residue):
    rows_block = 64
    total = query_act.shape[0]
    width = query_act.shape[1]
    modes = decay_rate.shape[0]
    blocks = total // rows_block
    live = token_mask.astype(jnp.float32)[:, None]
    inputs = live * key_act.astype(jnp.float32) * value_act.astype(jnp.float32)
    root_gain = jnp.sqrt(-jnp.expm1(-2.0 * decay_rate))
    filter_gain = residue * root_gain
    places = jnp.arange(rows_block).astype(jnp.float32)[:, None, None]
    rising = jnp.exp(decay_rate[None] * places)
    falling = jnp.exp(-decay_rate[None] * places)
    step_decay = jnp.exp(-decay_rate)
    trailing = jnp.exp(-decay_rate[None] * (rows_block - places))

    def forward_block(carried, block_in):
        scaled = rising * block_in[:, None, :]
        summed = jnp.cumsum(scaled, axis=0)
        states = falling * summed + falling * step_decay[None] * carried[None]
        return (states[-1], lax.optimization_barrier(jnp.sum(filter_gain[None] * states, axis=1)))
    zeros = jnp.zeros((modes, width), jnp.float32)
    _, conv = lax.scan(forward_block, zeros, inputs.reshape(blocks, rows_block, width))
    conv = conv.reshape(total, width)
    gate_grad = jnp.dot(out_grad, out_weight, preferred_element_type=jnp.float32)
    query_grad = (gate_grad * conv).astype(jnp.bfloat16)
    conv_grad = gate_grad * query_act.astype(jnp.float32)

    def backward_block(carry, block_in):
        carried, running = carry
        grad_blk, input_blk = block_in
        scaled = falling * grad_blk[:, None, :]
        summed = jnp.flip(jnp.cumsum(jnp.flip(scaled, 0), axis=0), 0)
        states = rising * summed + trailing * carried[None]
        running = running + lax.optimization_barrier(jnp.sum(input_blk[:, None, :] * states, axis=0))
        return ((states[0], running), lax.optimization_barrier(jnp.sum(filter_gain[None] * states, axis=1)))
    (_, running), input_grad = lax.scan(backward_block, (zeros, zeros), (conv_grad.reshape(blocks, rows_block, width), inputs.reshape(blocks, rows_block, width)), reverse=True)
    input_grad = input_grad.reshape(total, width)
    key_grad = (live * input_grad * value_act.astype(jnp.float32)).astype(jnp.bfloat16)
    value_grad = (live * input_grad * key_act.astype(jnp.float32)).astype(jnp.bfloat16)
    filter_grad = root_gain * running
    return (query_grad, key_grad, value_grad, filter_grad)
```

```python
import functools

import jax
import jax.numpy as jnp
from jax import lax
from jax.experimental import pallas as pl
from jax.experimental.pallas import tpu as pltpu
from jax.sharding import PartitionSpec as P


def carried_in(shard, axis, combine, identity, reverse):
    devices, here = (lax.axis_size(axis), lax.axis_index(axis))
    everything = jax.tree.map(lambda part: lax.all_gather(part, axis), shard)
    start = jax.tree.map(
        lambda part, zero: jnp.broadcast_to(jnp.asarray(zero, part.dtype), part.shape),
        shard,
        identity,
    )

    def turn(k, before):
        at = devices - 1 - k if reverse else k
        reached = at > here if reverse else at < here
        new = combine(before, jax.tree.map(lambda part: part[at], everything))
        return jax.tree.map(lambda a, b: jnp.where(reached, a, b), new, before)

    return lax.fori_loop(0, devices, turn, start)


def chain_join(earlier, later):
    return (earlier[0] * later[0], later[0] * earlier[1] + later[1])


ROWS = 64
TILE = 512


def scan_kernel(x_ref, g_ref, a_ref, gain_ref, fin_ref, bin_ref, conv_ref, igrad_ref, run_ref):
    tokens = x_ref.shape[0]
    blocks = tokens // ROWS
    modes = a_ref.shape[0]
    row = lax.broadcasted_iota(jnp.int32, (ROWS, ROWS), 0)
    col = lax.broadcasted_iota(jnp.int32, (ROWS, ROWS), 1)
    lower = (row >= col).astype(jnp.float32)
    upper = (row <= col).astype(jnp.float32)
    places = lax.broadcasted_iota(jnp.int32, (ROWS, 1), 0).astype(jnp.float32)
    conv_ref[...] = jnp.zeros_like(conv_ref)
    igrad_ref[...] = jnp.zeros_like(igrad_ref)

    def mode(m, _):
        a = a_ref[pl.ds(m, 1), :]
        gain = gain_ref[pl.ds(m, 1), :]
        rising = jnp.exp(a * places)
        falling = jnp.exp(-a * places)
        step = jnp.exp(-a)
        tail = jnp.exp(-a * float(ROWS))
        carried = fin_ref[pl.ds(m, 1), :]
        for b in range(blocks):
            xb = x_ref[pl.ds(b * ROWS, ROWS), :]
            summed = jnp.dot(lower, rising * xb, precision=lax.Precision.HIGHEST,
                             preferred_element_type=jnp.float32)
            states = falling * (summed + step * carried)
            conv_ref[pl.ds(b * ROWS, ROWS), :] += gain * states
            carried = states[ROWS - 1:ROWS, :]
        carried = bin_ref[pl.ds(m, 1), :]
        running = jnp.zeros_like(a)
        for b in reversed(range(blocks)):
            gb = g_ref[pl.ds(b * ROWS, ROWS), :]
            xb = x_ref[pl.ds(b * ROWS, ROWS), :]
            summed = jnp.dot(upper, falling * gb, precision=lax.Precision.HIGHEST,
                             preferred_element_type=jnp.float32)
            states = rising * (summed + tail * carried)
            running = running + jnp.sum(xb * states, axis=0, keepdims=True)
            igrad_ref[pl.ds(b * ROWS, ROWS), :] += gain * states
            carried = states[0:1, :]
        run_ref[pl.ds(m, 1), :] = running
        return 0

    lax.fori_loop(0, modes, mode, 0)


def local_scans(inputs, conv_grad, decay_rate, filter_gain, forward_in, backward_in):
    tokens, chans = inputs.shape
    modes = decay_rate.shape[0]
    tile = min(TILE, chans)
    seq = pl.BlockSpec((tokens, tile), lambda j: (0, j))
    par = pl.BlockSpec((modes, tile), lambda j: (0, j))
    return pl.pallas_call(
        scan_kernel,
        grid=(chans // tile,),
        in_specs=[seq, seq, par, par, par, par],
        out_specs=[seq, seq, par],
        out_shape=[
            jax.ShapeDtypeStruct((tokens, chans), jnp.float32),
            jax.ShapeDtypeStruct((tokens, chans), jnp.float32),
            jax.ShapeDtypeStruct((modes, chans), jnp.float32),
        ],
        compiler_params=pltpu.CompilerParams(dimension_semantics=("parallel",)),
    )(inputs, conv_grad, decay_rate, filter_gain, forward_in, backward_in)


def body(query_act, key_act, value_act, out_grad, out_weight, token_mask, decay_rate, residue):
    tokens_here = query_act.shape[0]
    live = token_mask.astype(jnp.float32)[:, None]
    inputs = live * key_act.astype(jnp.float32) * value_act.astype(jnp.float32)
    root_gain = jnp.sqrt(-jnp.expm1(-2.0 * decay_rate))
    filter_gain = residue * root_gain
    full_grad = lax.all_gather(out_grad, "ch", axis=1, tiled=True)
    gate_grad = jnp.dot(
        full_grad,
        lax.all_gather(out_weight, "ctx", axis=0, tiled=True),
        preferred_element_type=jnp.float32,
    )
    conv_grad = gate_grad * query_act.astype(jnp.float32)
    token_places = jnp.arange(tokens_here).astype(jnp.float32)[:, None, None]
    end_state = jnp.sum(
        jnp.exp(-decay_rate[None] * (tokens_here - 1.0 - token_places)) * inputs[:, None, :], axis=0
    )
    start_state = jnp.sum(
        jnp.exp(-decay_rate[None] * token_places) * conv_grad[:, None, :], axis=0
    )
    span_decay = jnp.exp(-decay_rate * tokens_here)
    zeros = jnp.zeros_like(decay_rate)
    forward_in = carried_in(
        (span_decay, end_state), "ctx", chain_join, (jnp.ones_like(span_decay), zeros), False
    )[1]
    backward_in = carried_in(
        (span_decay, start_state), "ctx", chain_join, (jnp.ones_like(span_decay), zeros), True
    )[1]
    conv, input_grad, running = local_scans(
        inputs, conv_grad, decay_rate, filter_gain, forward_in, backward_in
    )
    query_grad = (gate_grad * conv).astype(jnp.bfloat16)
    key_grad = (live * input_grad * value_act.astype(jnp.float32)).astype(jnp.bfloat16)
    value_grad = (live * input_grad * key_act.astype(jnp.float32)).astype(jnp.bfloat16)
    filter_grad = lax.psum(root_gain * running, "ctx")
    return (query_grad, key_grad, value_grad, filter_grad)


def solution(mesh):
    placed = (
        P("ctx", "ch"),
        P("ctx", "ch"),
        P("ctx", "ch"),
        P("ctx", "ch"),
        P("ctx", "ch"),
        P("ctx"),
        P(None, "ch"),
        P(None, "ch"),
    )
    return jax.shard_map(
        body,
        mesh=mesh,
        in_specs=placed,
        out_specs=(P("ctx", "ch"), P("ctx", "ch"), P("ctx", "ch"), P(None, "ch")),
        check_vma=False,
    )
```

```python
import jax
import jax.numpy as jnp
from jax import lax
from jax.experimental import pallas as pl
from jax.experimental.pallas import tpu as pltpu
from jax.sharding import PartitionSpec as P


ROWS = 64
TILE = 512


def scan_kernel(x_ref, g_ref, a_ref, gain_ref, fin_ref, bin_ref, conv_ref, igrad_ref, run_ref):
    tokens = x_ref.shape[0]
    blocks = tokens // ROWS
    modes = a_ref.shape[0]
    row = lax.broadcasted_iota(jnp.int32, (ROWS, ROWS), 0)
    col = lax.broadcasted_iota(jnp.int32, (ROWS, ROWS), 1)
    lower = (row >= col).astype(jnp.float32)
    upper = (row <= col).astype(jnp.float32)
    places = lax.broadcasted_iota(jnp.int32, (ROWS, 1), 0).astype(jnp.float32)
    conv_ref[...] = jnp.zeros_like(conv_ref)
    igrad_ref[...] = jnp.zeros_like(igrad_ref)

    def mode(m, _):
        a = a_ref[pl.ds(m, 1), :]
        gain = gain_ref[pl.ds(m, 1), :]
        rising = jnp.exp(a * places)
        falling = jnp.exp(-a * places)
        step = jnp.exp(-a)
        tail = jnp.exp(-a * float(ROWS))
        carried = fin_ref[pl.ds(m, 1), :]
        for b in range(blocks):
            xb = x_ref[pl.ds(b * ROWS, ROWS), :]
            summed = jnp.dot(lower, rising * xb, precision=lax.Precision.HIGHEST,
                             preferred_element_type=jnp.float32)
            states = falling * (summed + step * carried)
            conv_ref[pl.ds(b * ROWS, ROWS), :] += gain * states
            carried = states[ROWS - 1:ROWS, :]
        carried = bin_ref[pl.ds(m, 1), :]
        running = jnp.zeros_like(a)
        for b in reversed(range(blocks)):
            gb = g_ref[pl.ds(b * ROWS, ROWS), :]
            xb = x_ref[pl.ds(b * ROWS, ROWS), :]
            summed = jnp.dot(upper, falling * gb, precision=lax.Precision.HIGHEST,
                             preferred_element_type=jnp.float32)
            states = rising * (summed + tail * carried)
            running = running + jnp.sum(xb * states, axis=0, keepdims=True)
            igrad_ref[pl.ds(b * ROWS, ROWS), :] += gain * states
            carried = states[0:1, :]
        run_ref[pl.ds(m, 1), :] = running
        return 0

    lax.fori_loop(0, modes, mode, 0)


def local_scans(inputs, conv_grad, decay_rate, filter_gain, forward_in, backward_in):
    tokens, chans = inputs.shape
    modes = decay_rate.shape[0]
    tile = min(TILE, chans)
    seq = pl.BlockSpec((tokens, tile), lambda j: (0, j))
    par = pl.BlockSpec((modes, tile), lambda j: (0, j))
    return pl.pallas_call(
        scan_kernel,
        grid=(chans // tile,),
        in_specs=[seq, seq, par, par, par, par],
        out_specs=[seq, seq, par],
        out_shape=[
            jax.ShapeDtypeStruct((tokens, chans), jnp.float32),
            jax.ShapeDtypeStruct((tokens, chans), jnp.float32),
            jax.ShapeDtypeStruct((modes, chans), jnp.float32),
        ],
        compiler_params=pltpu.CompilerParams(dimension_semantics=("parallel",)),
    )(inputs, conv_grad, decay_rate, filter_gain, forward_in, backward_in)


def body(query_act, key_act, value_act, out_grad, out_weight, token_mask, decay_rate, residue):
    tokens_here = query_act.shape[0]
    live = token_mask.astype(jnp.float32)[:, None]
    inputs = live * key_act.astype(jnp.float32) * value_act.astype(jnp.float32)
    root_gain = jnp.sqrt(-jnp.expm1(-2.0 * decay_rate))
    filter_gain = residue * root_gain
    full_grad = lax.all_gather(out_grad, "ch", axis=1, tiled=True)
    gate_grad = jnp.dot(
        full_grad,
        lax.all_gather(out_weight, "ctx", axis=0, tiled=True),
        preferred_element_type=jnp.float32,
    )
    conv_grad = gate_grad * query_act.astype(jnp.float32)
    token_places = jnp.arange(tokens_here).astype(jnp.float32)[:, None, None]
    end_state = jnp.sum(
        jnp.exp(-decay_rate[None] * (tokens_here - 1.0 - token_places)) * inputs[:, None, :], axis=0
    )
    start_state = jnp.sum(
        jnp.exp(-decay_rate[None] * token_places) * conv_grad[:, None, :], axis=0
    )
    span_decay = jnp.exp(-decay_rate * tokens_here)
    everything = lax.all_gather(jnp.stack([span_decay, end_state, start_state]), "ctx")
    devices, here = (lax.axis_size("ctx"), lax.axis_index("ctx"))
    forward_in = jnp.zeros_like(decay_rate)
    for k in range(devices):
        joined = everything[k, 0] * forward_in + everything[k, 1]
        forward_in = jnp.where(k < here, joined, forward_in)
    backward_in = jnp.zeros_like(decay_rate)
    for k in reversed(range(devices)):
        joined = everything[k, 0] * backward_in + everything[k, 2]
        backward_in = jnp.where(k > here, joined, backward_in)
    conv, input_grad, running = local_scans(
        inputs, conv_grad, decay_rate, filter_gain, forward_in, backward_in
    )
    query_grad = (gate_grad * conv).astype(jnp.bfloat16)
    key_grad = (live * input_grad * value_act.astype(jnp.float32)).astype(jnp.bfloat16)
    value_grad = (live * input_grad * key_act.astype(jnp.float32)).astype(jnp.bfloat16)
    filter_grad = lax.psum(root_gain * running, "ctx")
    return (query_grad, key_grad, value_grad, filter_grad)


def solution(mesh):
    placed = (
        P("ctx", "ch"),
        P("ctx", "ch"),
        P("ctx", "ch"),
        P("ctx", "ch"),
        P("ctx", "ch"),
        P("ctx"),
        P(None, "ch"),
        P(None, "ch"),
    )
    return jax.shard_map(
        body,
        mesh=mesh,
        in_specs=placed,
        out_specs=(P("ctx", "ch"), P("ctx", "ch"), P("ctx", "ch"), P(None, "ch")),
        check_vma=False,
    )
```

```python
import jax
import jax.numpy as jnp
from jax import lax
from jax.experimental import pallas as pl
from jax.experimental.pallas import tpu as pltpu
from jax.sharding import PartitionSpec as P


ROWS = 64
TILE = 512


def scan_kernel(x_ref, g_ref, a_ref, gain_ref, fin_ref, bin_ref, conv_ref, igrad_ref, run_ref):
    tokens = x_ref.shape[0]
    blocks = tokens // ROWS
    modes = a_ref.shape[0]
    row = lax.broadcasted_iota(jnp.int32, (ROWS, ROWS), 0)
    col = lax.broadcasted_iota(jnp.int32, (ROWS, ROWS), 1)
    lower = (row >= col).astype(jnp.float32)
    upper = (row <= col).astype(jnp.float32)
    places = lax.broadcasted_iota(jnp.int32, (ROWS, 1), 0).astype(jnp.float32)
    conv_ref[...] = jnp.zeros_like(conv_ref)
    igrad_ref[...] = jnp.zeros_like(igrad_ref)

    def mode(m, _):
        a = a_ref[pl.ds(m, 1), :]
        gain = gain_ref[pl.ds(m, 1), :]
        rising = jnp.exp(a * places)
        falling = jnp.exp(-a * places)
        step = jnp.exp(-a)
        tail = jnp.exp(-a * float(ROWS))
        carried = fin_ref[pl.ds(m, 1), :]
        for b in range(blocks):
            xb = x_ref[pl.ds(b * ROWS, ROWS), :]
            summed = jnp.dot(lower, rising * xb, precision=lax.Precision.HIGHEST,
                             preferred_element_type=jnp.float32)
            states = falling * (summed + step * carried)
            conv_ref[pl.ds(b * ROWS, ROWS), :] += gain * states
            carried = states[ROWS - 1:ROWS, :]
        carried = bin_ref[pl.ds(m, 1), :]
        running = jnp.zeros_like(a)
        for b in reversed(range(blocks)):
            gb = g_ref[pl.ds(b * ROWS, ROWS), :]
            xb = x_ref[pl.ds(b * ROWS, ROWS), :]
            summed = jnp.dot(upper, falling * gb, precision=lax.Precision.HIGHEST,
                             preferred_element_type=jnp.float32)
            states = rising * (summed + tail * carried)
            running = running + jnp.sum(xb * states, axis=0, keepdims=True)
            igrad_ref[pl.ds(b * ROWS, ROWS), :] += gain * states
            carried = states[0:1, :]
        run_ref[pl.ds(m, 1), :] = running
        return 0

    lax.fori_loop(0, modes, mode, 0)


def local_scans(inputs, conv_grad, decay_rate, filter_gain, forward_in, backward_in):
    tokens, chans = inputs.shape
    modes = decay_rate.shape[0]
    tile = min(TILE, chans)
    seq = pl.BlockSpec((tokens, tile), lambda j: (0, j))
    par = pl.BlockSpec((modes, tile), lambda j: (0, j))
    return pl.pallas_call(
        scan_kernel,
        grid=(chans // tile,),
        in_specs=[seq, seq, par, par, par, par],
        out_specs=[seq, seq, par],
        out_shape=[
            jax.ShapeDtypeStruct((tokens, chans), jnp.float32),
            jax.ShapeDtypeStruct((tokens, chans), jnp.float32),
            jax.ShapeDtypeStruct((modes, chans), jnp.float32),
        ],
        compiler_params=pltpu.CompilerParams(dimension_semantics=("parallel",)),
    )(inputs, conv_grad, decay_rate, filter_gain, forward_in, backward_in)


def body(query_act, key_act, value_act, out_grad, out_weight, token_mask, decay_rate, residue):
    tokens_here = query_act.shape[0]
    live = token_mask.astype(jnp.float32)[:, None]
    inputs = live * key_act.astype(jnp.float32) * value_act.astype(jnp.float32)
    root_gain = jnp.sqrt(-jnp.expm1(-2.0 * decay_rate))
    filter_gain = residue * root_gain
    full_grad = lax.all_gather(out_grad, "ch", axis=1, tiled=True)
    gate_grad = jnp.dot(
        full_grad,
        lax.all_gather(out_weight, "ctx", axis=0, tiled=True),
        preferred_element_type=jnp.float32,
    )
    conv_grad = gate_grad * query_act.astype(jnp.float32)
    token_places = jnp.arange(tokens_here).astype(jnp.float32)[:, None, None]
    end_state = jnp.sum(
        jnp.exp(-decay_rate[None] * (tokens_here - 1.0 - token_places)) * inputs[:, None, :], axis=0
    )
    start_state = jnp.sum(
        jnp.exp(-decay_rate[None] * token_places) * conv_grad[:, None, :], axis=0
    )
    span_decay = jnp.exp(-decay_rate * tokens_here)
    everything = lax.all_gather(jnp.stack([span_decay, end_state, start_state]), "ctx")
    devices, here = (lax.axis_size("ctx"), lax.axis_index("ctx"))
    forward_in = jnp.zeros_like(decay_rate)
    for k in range(devices):
        joined = everything[k, 0] * forward_in + everything[k, 1]
        forward_in = jnp.where(k < here, joined, forward_in)
    backward_in = jnp.zeros_like(decay_rate)
    for k in reversed(range(devices)):
        joined = everything[k, 0] * backward_in + everything[k, 2]
        backward_in = jnp.where(k > here, joined, backward_in)
    conv, input_grad, running = local_scans(
        inputs, conv_grad, decay_rate, filter_gain, forward_in, backward_in
    )
    query_grad = (gate_grad * conv).astype(jnp.bfloat16)
    key_grad = (live * input_grad * value_act.astype(jnp.float32)).astype(jnp.bfloat16)
    value_grad = (live * input_grad * key_act.astype(jnp.float32)).astype(jnp.bfloat16)
    filter_grad = jnp.sum(lax.all_gather(root_gain * running, "ctx"), axis=0)
    return (query_grad, key_grad, value_grad, filter_grad)


def solution(mesh):
    placed = (
        P("ctx", "ch"),
        P("ctx", "ch"),
        P("ctx", "ch"),
        P("ctx", "ch"),
        P("ctx", "ch"),
        P("ctx"),
        P(None, "ch"),
        P(None, "ch"),
    )
    return jax.shard_map(
        body,
        mesh=mesh,
        in_specs=placed,
        out_specs=(P("ctx", "ch"), P("ctx", "ch"), P("ctx", "ch"), P(None, "ch")),
        check_vma=False,
    )
```
